32 devices in a mesh: groups: 2 (over y), sub: 16 (over z, x, core).
Axes of the slice: x: 2, y: 2, z: 4, core: 2. Of those that a mesh axis runs over, the one named last changes fastest.
Arguments:
- modes: bfloat16 [65536, 512], P(('groups', 'sub')), parts along dimension 0, may hold values from -0.5 to 0.5
- eigenvalues: float32 [32, 512], P(('groups', 'sub')), parts along dimension 0, may hold values from 2 to 20
- sub_size: int32 [32], P(('groups', 'sub')), parts along dimension 0, may hold values from 1024 to 2048
- row_offset: int32 [1024, 128], P(('groups', 'sub')), parts along dimension 0, may hold values from 0 to 1023
- stiff_coupling: bfloat16 [1024, 128, 128], P(('groups', 'sub')), parts along dimension 0, may hold values from -0.29882812 to 0.29882812
- iface_offset: int32 [1024], P(('groups', 'sub')), parts along dimension 0, may hold values from 0 to 6
- stiff_iface: float32 [32, 128, 128], P(('groups', 'sub')), parts along dimension 0, may hold values from -18 to 18
- lumped_mass: float32 [32, 128], P(('groups', 'sub')), parts along dimension 0, may hold values from 0.5 to 5
Outputs:
- reduced: float32 [32, 128, 128], P(('groups', 'sub')), parts along dimension 0
- factor: float32 [32, 128, 128], P(('groups', 'sub')), parts along dimension 0
- coupled: bfloat16 [1024, 512, 128], P(('groups', 'sub')), parts along dimension 0
The draws below stay inside these ranges and needn't reach their ends.
There are 2 independent parts, one for each index of `groups`. The reference program is written for one: setup_inputs(seed, part) draws one part's arguments, and reference() takes and returns one part's arrays. A program takes and returns all parts, laid end to end along the dimension named above; each array names one. Nothing has to cross between parts.
Inputs may be any that keep to these rules, and one draw needn't show every extreme that they name: Block b of substructure s belongs to interface (s + iface_offset[b] - 3) mod 16, so a substructure's interfaces lie within 3 places of it in substructure order.
All inputs are finite; a program needn't handle non-finite values.
Results may differ from the reference program's by a relative error of at most 0.001.
The reference program's roundings to bfloat16 on the way (of `projected`) count: a program that leaves them out, or rounds other values in their place, can miss the bound.
Values sent between devices are 32-bit elements; how exact they have to be, the bound alone decides.
No kernel may reach another device: no remote copies, remote signals or barrier semaphores. Data moves between devices by JAX's collectives and lax.ppermute only.
A program may use at most 64 MiB of HBM per device.

```python
import math
import jax
import jax.numpy as jnp
import numpy as np
from jax import lax

M = 512
IB = 128
CR = 128
NMAX = 2048
NB = 32
REACH = 3
N_SUB = 16


def with_ends(drawn, rng, low, largest):
    spot = [jax.random.randint(jax.random.fold_in(rng, axis), (), 0, length) for axis, length in enumerate(drawn.shape)]
    longest = drawn.shape.index(max(drawn.shape))
    next_to = spot[:longest] + [(spot[longest] + 1) % drawn.shape[longest]] + spot[longest + 1:]
    return drawn.at[tuple(spot)].set(low).at[tuple(next_to)].set(largest)


def block_levels(stream_key, dims, split, least, high):
    level = 1.0
    for axis_at, shards_of in split:
        draws = jax.random.uniform(jax.random.fold_in(jax.random.fold_in(stream_key, 6), axis_at), (shards_of,), jnp.float32, least / len(split), high / len(split))
        level = level * jnp.repeat(jnp.exp(draws), dims[axis_at] // shards_of).reshape((-1,) + (1,) * (len(dims) - 1 - axis_at))
    return level


def rank_table(count, lean):
    portions = [(1 << 20) // math.isqrt(standing ** lean) + 1 for standing in range(1, count + 1)]
    deviation = 1 + sum(portions) // (1 << 30)
    return np.cumsum(np.array([max(1, weight // deviation) for weight in portions]))


def skewed_ids(stream_key, extent, number_of, skew):
    table = rank_table(number_of, skew)
    pick = jax.random.randint(jax.random.fold_in(stream_key, 1), extent, 0, int(table[number_of - 1]))
    standing = jnp.searchsorted(jnp.asarray(table, jnp.int32), pick, side="right")
    return jax.random.permutation(jax.random.fold_in(stream_key, 2), number_of)[standing].astype(jnp.int32)


def bell_draw(stream_key, dims, width, limit, shards=(), held_as=jnp.bfloat16):
    values = jax.random.normal(stream_key, dims, jnp.float32) * width
    if len(shards) > 0:
        values = block_levels(stream_key, dims, shards, -0.22, 0.18) * values
    return jnp.clip(values, min=-limit, max=limit).astype(held_as)


def setup_inputs(seed: int = 0, part: int = 0) -> dict:
    arg_keys = jax.random.split(jax.random.key(seed), 9)
    part_splits = jax.random.split(jax.random.fold_in(arg_keys[8], part), 9)
    modes = bell_draw(part_splits[0], (N_SUB * NMAX, M), CR ** -0.5, 0.5, ((0, 16),))
    eigenvalues = jnp.clip(jnp.exp(math.log(20.0) - 2.3025851 * jax.random.uniform(part_splits[1], (N_SUB, M), jnp.float32) ** block_levels(part_splits[1], (N_SUB, M), ((0, 16),), -0.2, 0.2)), 2.0, 20.0)
    sub_size = with_ends(jax.random.randint(part_splits[2], (N_SUB,), NMAX // 2, NMAX + 1), jax.random.fold_in(part_splits[2], 1), NMAX // 2, NMAX).astype(jnp.int32)
    row_offset = with_ends(jax.random.randint(part_splits[3], (N_SUB * NB, CR), 0, NMAX // 2), jax.random.fold_in(part_splits[3], 1), 0, (NMAX // 2) - 1).astype(jnp.int32)
    stiff_coupling = bell_draw(part_splits[4], (N_SUB * NB, CR, IB), 0.05, 0.29882812, ((0, 16),))
    iface_offset = with_ends(skewed_ids(part_splits[5], (N_SUB * NB,), 2 * REACH + 1, 2), jax.random.fold_in(part_splits[5], 3), 0, 2 * REACH).astype(jnp.int32)
    stiff_iface = bell_draw(part_splits[6], (N_SUB, IB, IB), 3.0, 18.0, ((0, 16),), jnp.float32)
    lumped_mass = jnp.clip(jnp.exp(math.log(5.0) - 2.3025851 * jax.random.uniform(part_splits[7], (N_SUB, IB), jnp.float32) ** block_levels(part_splits[7], (N_SUB, IB), ((0, 16),), -0.2, 0.2)), 0.5, 5.0)
    return {"modes": modes, "eigenvalues": eigenvalues, "sub_size": sub_size, "row_offset": row_offset, "stiff_coupling": stiff_coupling, "iface_offset": iface_offset, "stiff_iface": stiff_iface, "lumped_mass": lumped_mass}


def project(modes_block, size_value, offsets, coupling):
    picked_rows = (size_value - 1 - offsets).astype(jnp.int32)
    picked = jnp.take(modes_block, picked_rows, axis=0).astype(jnp.float32)
    return jnp.einsum('brm,bri->bmi', picked, coupling.astype(jnp.float32)).astype(jnp.bfloat16)

def schur_terms(projected, eigen_row):
    widened = projected.astype(jnp.float32)
    inverse = 1.0 / eigen_row
    stiff_part = jnp.einsum('bmi,bmj->bij', widened * inverse[None, :, None], widened, precision=lax.Precision.HIGHEST)
    mass_part = jnp.einsum('bmi,bmj->bij', widened * (inverse * inverse)[None, :, None], widened, precision=lax.Precision.HIGHEST)
    return (stiff_part, mass_part)

def reference(modes, eigenvalues, sub_size, row_offset, stiff_coupling, iface_offset, stiff_iface, lumped_mass):
    modes_all = modes.reshape(N_SUB, NMAX, M)
    offsets_all = row_offset.reshape(N_SUB, NB, CR)
    coupling_all = stiff_coupling.reshape(N_SUB, NB, CR, IB)
    owners_row = jnp.arange(N_SUB, dtype=jnp.int32)[:, None]
    targets = ((iface_offset.reshape(N_SUB, NB) - REACH + owners_row) % N_SUB).astype(jnp.int32)

    def accumulate(totals, inputs):
        modes_block, size_value, offsets, coupling, eigen_row, target_row = inputs
        projected = project(modes_block, size_value, offsets, coupling)
        stiff_part, mass_part = schur_terms(projected, eigen_row)
        return ((totals[0].at[target_row].add(stiff_part), totals[1].at[target_row].add(mass_part)), None)
    zeros_block = jnp.zeros((N_SUB, IB, IB), jnp.float32)
    (stiff_sum, mass_sum), _ = lax.scan(accumulate, (zeros_block, zeros_block), (modes_all, sub_size, offsets_all, coupling_all, eigenvalues, targets))
    reduced = stiff_iface - stiff_sum
    identity = jnp.eye(IB, dtype=jnp.float32)
    mass_matrix = mass_sum + lumped_mass[:, :, None] * identity[None]
    factor = jnp.linalg.cholesky(mass_matrix)
    inverse_factor = lax.linalg.triangular_solve(factor, jnp.broadcast_to(identity, factor.shape), left_side=True, lower=True)

    def transform(inputs):
        modes_block, size_value, offsets, coupling, target_row = inputs
        projected = project(modes_block, size_value, offsets, coupling).astype(jnp.float32)
        chosen = inverse_factor[target_row]
        solved = jnp.einsum('bmi,bji->bmj', projected, chosen, precision=lax.Precision.HIGHEST)
        return solved.astype(jnp.bfloat16)
    coupled = lax.map(transform, (modes_all, sub_size, offsets_all, coupling_all, targets))
    return (reduced, factor, coupled.reshape(N_SUB * NB, M, IB))
```

```python
import jax
import jax.numpy as jnp
from jax import lax
from jax.experimental import pallas as pl
from jax.experimental.pallas import tpu as pltpu
from jax.sharding import PartitionSpec as P

REACH = 3
NEAR = 2 * REACH + 1
GROUP = 4
ROWS = 8
TILE = 16
F32 = jnp.float32
BF16 = jnp.bfloat16
DISTANCES = tuple(d for d in range(-REACH, REACH + 1) if d != 0)


def passed_along(x, axis, by):
    length = lax.axis_size(axis)
    return lax.ppermute(x, axis, [(i, (i + by) % length) for i in range(length)])


def halves(x):
    high = x.astype(BF16)
    return high, (x - high.astype(F32)).astype(BF16)


def dot(a, b, contract=(1, 0)):
    return lax.dot_general(
        a, b, (((contract[0],), (contract[1],)), ((), ())), preferred_element_type=F32
    )


def iotas(shape):
    return (
        lax.broadcasted_iota(jnp.int32, shape, 0),
        lax.broadcasted_iota(jnp.int32, shape, 1),
    )


def project_kernel(
    size, offset, modes, eigen, row_offset, coupling,
    projected, *rest,
):
    packed = rest[:NEAR]
    window, turned, weights, sums, arrived = rest[NEAR:]
    step = pl.program_id(0)
    width = coupling.shape[2]
    picks = coupling.shape[1]
    span = turned.shape[1]

    @pl.when(step == 0)
    def _():
        start = size[0] - span
        base = jnp.minimum(start // TILE * TILE, modes.shape[0] - window.shape[0])
        copy = pltpu.make_async_copy(
            modes.at[pl.ds(pl.multiple_of(base, TILE), window.shape[0]), :], window, arrived
        )
        copy.start()
        sums[...] = jnp.zeros_like(sums)
        inverse = 1.0 / eigen[...]
        weights[0:1, :] = inverse * inverse
        weights[1:2, :] = inverse
        copy.wait()
        moved = pltpu.roll(
            window[...].astype(F32), window.shape[0] - (start - base), 0
        )
        turned[...] = moved[:span].T.astype(BF16)

    place, _ = iotas((span, GROUP * picks))
    wanted = jnp.concatenate(
        [span - 1 - row_offset[pl.ds(step * GROUP + g, 1), :] for g in range(GROUP)], axis=1
    )
    chosen = jnp.where(place == wanted, 1.0, 0.0).astype(BF16)
    picked = dot(turned[...], chosen).astype(BF16)
    for g in range(GROUP):
        mine = picked[:, g * picks : (g + 1) * picks]
        block = dot(mine, coupling[g]).astype(BF16)
        projected[g] = block
        across = dot(coupling[g], mine, (0, 1)).astype(BF16).astype(F32)
        mass = halves(across * weights[0:1, :])
        stiff = halves(across * weights[1:2, :])
        terms = dot(jnp.concatenate([*mass, *stiff], axis=0), block)
        where = offset[step * GROUP + g]
        sums[where, 0] += terms[:width] + terms[width : 2 * width]
        sums[where, 1] += terms[2 * width : 3 * width] + terms[3 * width :]

    @pl.when(step == pl.num_programs(0) - 1)
    def _():
        row, column = iotas((width, width))
        for k in range(NEAR):
            stiff = sums[k, 1]
            packed[k][0:width, :] = jnp.where(row >= column, sums[k, 0], stiff)
            diagonal = jnp.sum(jnp.where(row == column, stiff, 0.0), axis=0, keepdims=True)
            packed[k][width:, :] = jnp.broadcast_to(diagonal, (ROWS, width))


def factor_kernel(*refs):
    received = refs[:NEAR]
    stiff_iface, lumped, reduced, factor, inverse = refs[NEAR:]
    width = lumped.shape[1]
    total = received[0][...]
    for piece in received[1:]:
        total = total + piece[...]
    row, column = iotas((width, width))
    upper = jnp.where(row < column, total[:width], 0.0)
    on_diagonal = jnp.where(row == column, total[width : width + 1, :], 0.0)
    reduced[0] = stiff_iface[0] - (upper + upper.T + on_diagonal)
    lower = jnp.where(row > column, total[:width], 0.0)
    on_diagonal = jnp.where(row == column, total[:width] + lumped[...], 0.0)
    mass = lower + lower.T + on_diagonal
    identity = jnp.where(row == column, 1.0, 0.0)
    panels = width // ROWS
    left = [mass[p * ROWS : (p + 1) * ROWS] for p in range(panels)]
    right = [identity[p * ROWS : (p + 1) * ROWS] for p in range(panels)]
    spread = (ROWS, width)
    for p in range(panels):
        at = p * ROWS
        columns = [
            jnp.broadcast_to(left[p][:, at + j : at + j + 1], spread) for j in range(ROWS)
        ]
        pivot = {
            (i, j): jnp.broadcast_to(columns[j][i : i + 1, :], spread)
            for j in range(ROWS)
            for i in range(j, ROWS)
        }
        scale = []
        for j in range(ROWS):
            scale.append(lax.rsqrt(pivot[j, j]))
            for i in range(j + 1, ROWS):
                pivot[i, j] = pivot[i, j] * scale[j]
            for k in range(j + 1, ROWS):
                for i in range(k, ROWS):
                    pivot[i, k] = pivot[i, k] - pivot[i, j] * pivot[k, j]
        solved_left, solved_right = [], []
        for j in range(ROWS):
            a = jnp.broadcast_to(left[p][j : j + 1, :], spread)
            x = jnp.broadcast_to(right[p][j : j + 1, :], spread)
            for k in range(j):
                a = a - pivot[j, k] * solved_left[k]
                x = x - pivot[j, k] * solved_right[k]
            solved_left.append(a * scale[j])
            solved_right.append(x * scale[j])
        for q in range(p + 1, panels):
            below = []
            for j in range(ROWS):
                v = jnp.broadcast_to(left[q][:, at + j : at + j + 1], spread)
                for k in range(j):
                    v = v - pivot[j, k] * below[k]
                below.append(v * scale[j])
            for j in range(ROWS):
                left[q] = left[q] - below[j] * solved_left[j]
                right[q] = right[q] - below[j] * solved_right[j]
        line, _ = iotas(spread)
        kept_left, kept_right = solved_left[0], solved_right[0]
        for j in range(1, ROWS):
            kept_left = jnp.where(line == j, solved_left[j], kept_left)
            kept_right = jnp.where(line == j, solved_right[j], kept_right)
        left[p], right[p] = kept_left, kept_right
    inverse[...] = jnp.where(row >= column, jnp.concatenate(right, axis=0), 0.0)
    factor[0] = jnp.where(row <= column, jnp.concatenate(left, axis=0), 0.0).T


def transform_kernel(offset, projected, *refs):
    pieces = refs[:NEAR]
    coupled, split = refs[NEAR:]
    step = pl.program_id(0)
    width = projected.shape[2]

    @pl.when(step == 0)
    def _():
        for k in range(NEAR):
            high, low = halves(pieces[k][...])
            split[k, :, 0:width] = high
            split[k, :, width:] = low

    for g in range(GROUP):
        where = offset[step * GROUP + g]
        twice = jnp.concatenate([projected[g], projected[g]], axis=1)
        coupled[g] = dot(twice, split[where], (1, 1)).astype(BF16)


def in_smem():
    return pl.BlockSpec(memory_space=pltpu.SMEM)


def in_vmem():
    return pl.BlockSpec(memory_space=pltpu.VMEM)


def per_device(
    modes, eigenvalues, sub_size, row_offset, stiff_coupling, iface_offset, stiff_iface, lumped_mass
):
    blocks, picks, width = stiff_coupling.shape
    rows, kept = modes.shape
    span = rows // 2
    by_group = pl.BlockSpec((GROUP, kept, width), lambda i: (i, 0, 0))
    projected, *sums = pl.pallas_call(
        project_kernel,
        grid=(blocks // GROUP,),
        in_specs=[
            in_smem(),
            in_smem(),
            pl.BlockSpec(memory_space=pl.ANY),
            in_vmem(),
            in_vmem(),
            pl.BlockSpec((GROUP, picks, width), lambda i: (i, 0, 0)),
        ],
        out_specs=[by_group] + [in_vmem()] * NEAR,
        out_shape=[jax.ShapeDtypeStruct((blocks, kept, width), BF16)]
        + [jax.ShapeDtypeStruct((width + ROWS, width), F32)] * NEAR,
        scratch_shapes=[
            pltpu.VMEM((span + TILE, kept), BF16),
            pltpu.VMEM((kept, span), BF16),
            pltpu.VMEM((8, kept), F32),
            pltpu.VMEM((NEAR, 2, width, width), F32),
            pltpu.SemaphoreType.DMA(()),
        ],
        compiler_params=pltpu.CompilerParams(dimension_semantics=("arbitrary",)),
        name="project",
    )(sub_size, iface_offset, modes, eigenvalues, row_offset, stiff_coupling)
    received = [sums[REACH]] + [passed_along(sums[d + REACH], "sub", d) for d in DISTANCES]
    reduced, factor, inverse = pl.pallas_call(
        factor_kernel,
        in_specs=[in_vmem()] * (NEAR + 2),
        out_specs=[in_vmem()] * 3,
        out_shape=[
            jax.ShapeDtypeStruct((1, width, width), F32),
            jax.ShapeDtypeStruct((1, width, width), F32),
            jax.ShapeDtypeStruct((width, width), F32),
        ],
        name="factor",
    )(*received, stiff_iface, lumped_mass)
    pieces = [
        inverse if d == 0 else passed_along(inverse, "sub", -d) for d in range(-REACH, REACH + 1)
    ]
    coupled = pl.pallas_call(
        transform_kernel,
        grid=(blocks // GROUP,),
        in_specs=[in_smem(), by_group] + [in_vmem()] * NEAR,
        out_specs=by_group,
        out_shape=jax.ShapeDtypeStruct((blocks, kept, width), BF16),
        scratch_shapes=[pltpu.VMEM((NEAR, width, 2 * width), BF16)],
        compiler_params=pltpu.CompilerParams(dimension_semantics=("arbitrary",)),
        name="transform",
    )(iface_offset, projected, *pieces)
    return (reduced, factor, coupled)


def solution(mesh):
    placed = (
        P(("groups", "sub"), None),
        P(("groups", "sub"), None),
        P(("groups", "sub")),
        P(("groups", "sub"), None),
        P(("groups", "sub"), None, None),
        P(("groups", "sub")),
        P(("groups", "sub"), None, None),
        P(("groups", "sub"), None),
    )
    return jax.shard_map(
        per_device,
        mesh=mesh,
        in_specs=placed,
        out_specs=(
            P(("groups", "sub"), None, None),
            P(("groups", "sub"), None, None),
            P(("groups", "sub"), None, None),
        ),
        check_vma=False,
    )
```

```python
import jax
import jax.numpy as jnp
from jax import lax
from jax.experimental import pallas as pl
from jax.experimental.pallas import tpu as pltpu
from jax.sharding import PartitionSpec as P

REACH = 3
NEAR = 2 * REACH + 1
GROUP = 4
ROWS = 8
PARTS = 4
TILE = 16
VMEM_LIMIT = 24 << 20
F32 = jnp.float32
BF16 = jnp.bfloat16
DISTANCES = tuple(d for d in range(-REACH, REACH + 1) if d != 0)


def passed_along(x, axis, by):
    length = lax.axis_size(axis)
    moved = lax.ppermute(x, axis, [(i, (i + by) % length) for i in range(length)])
    return pltpu.with_memory_space_constraint(moved, pltpu.VMEM)


def halves(x):
    high = x.astype(BF16)
    return high, (x - high.astype(F32)).astype(BF16)


def dot(a, b, contract=(1, 0)):
    return lax.dot_general(
        a, b, (((contract[0],), (contract[1],)), ((), ())), preferred_element_type=F32
    )


def iotas(shape):
    return (
        lax.broadcasted_iota(jnp.int32, shape, 0),
        lax.broadcasted_iota(jnp.int32, shape, 1),
    )


def project_kernel(size, offset, modes, eigen, row_offset, coupling, turned, *rest):
    packed = rest[:NEAR]
    offsets, rows, values, wants, blocks_in, span_rows, picked, sums, arrived = rest[NEAR:]
    blocks, picks, width = coupling.shape
    span = span_rows.shape[0]
    part = rows.shape[0] // PARTS
    pairs = [(row_offset, wants), (offset, offsets), (eigen, values)]
    pairs += [
        (modes.at[pl.ds(k * part, part), :], rows.at[pl.ds(k * part, part), :])
        for k in range(PARTS)
    ]
    pairs.append((coupling, blocks_in))
    copies = [
        pltpu.make_async_copy(source, target, arrived.at[k])
        for k, (source, target) in enumerate(pairs)
    ]
    for copy in copies:
        copy.start()
    sums[...] = jnp.zeros_like(sums)
    _, place = iotas((picks, span))
    for copy in copies[:3]:
        copy.wait()
    wanted = (span - 1 - wants[...]).T
    inverse = 1.0 / values[...]
    weight = inverse * inverse
    start = size[0] - span
    base = jnp.minimum(start // TILE * TILE, rows.shape[0] - span - TILE)
    for copy in copies[3:]:
        copy.wait()
    window = rows[pl.ds(pl.multiple_of(base, TILE), span + TILE), :].astype(F32)
    moved = pltpu.roll(window, span + TILE - (start - base), 0)
    span_rows[...] = moved[:span].astype(BF16)
    groups = blocks // GROUP
    for i in range(groups + 2):
        if i >= 2:
            for b in range((i - 2) * GROUP, (i - 1) * GROUP):
                block = turned[b]
                mass = halves(block.astype(F32) * weight)
                terms = dot(jnp.concatenate(mass, axis=0), block, (1, 1))
                sums[offsets[b]] += terms[:width] + terms[width:]
        if 1 <= i <= groups:
            for g in range(GROUP):
                b = (i - 1) * GROUP + g
                mine = picked[(i - 1) % 2, g * picks : (g + 1) * picks, :]
                turned[b] = dot(blocks_in[b].T, mine).astype(BF16)
        if i < groups:
            chosen = [
                jnp.where(place == wanted[:, b : b + 1], 1.0, 0.0).astype(BF16)
                for b in range(i * GROUP, (i + 1) * GROUP)
            ]
            picked[i % 2] = dot(jnp.concatenate(chosen, axis=0), span_rows[...]).astype(BF16)
    for k in range(NEAR):
        packed[k][...] = sums[k]


def stiffen_kernel(offset, eigen, turned, projected, sums):
    width = sums.shape[1]
    sums[...] = jnp.zeros_like(sums)
    weight = 1.0 / eigen[...]
    for b in range(turned.shape[0]):
        block = turned[b]
        stiff = halves(block.astype(F32) * weight)
        terms = dot(jnp.concatenate(stiff, axis=0), block, (1, 1))
        sums[offset[b]] += terms[:width] + terms[width:]
        projected[b] = block.T


def factor_kernel(*refs):
    received = refs[:NEAR]
    lumped, stiff, factor = refs[NEAR : NEAR + 3]
    parcels = refs[NEAR + 3 :]
    width = lumped.shape[1]
    total = received[0][...]
    for piece in received[1:]:
        total = total + piece[...]
    row, column = iotas((width, width))
    lower = jnp.where(row > column, total, 0.0)
    mass = lower + lower.T + jnp.where(row == column, total + lumped[...], 0.0)
    identity = jnp.where(row == column, 1.0, 0.0)
    panels = width // ROWS
    left = [mass[p * ROWS : (p + 1) * ROWS] for p in range(panels)]
    right = [identity[p * ROWS : (p + 1) * ROWS] for p in range(panels)]
    spread = (ROWS, width)
    for p in range(panels):
        at = p * ROWS
        columns = [
            jnp.broadcast_to(left[p][:, at + j : at + j + 1], spread) for j in range(ROWS)
        ]
        pivot = {
            (i, j): jnp.broadcast_to(columns[j][i : i + 1, :], spread)
            for j in range(ROWS)
            for i in range(j, ROWS)
        }
        scale = []
        for j in range(ROWS):
            scale.append(lax.rsqrt(pivot[j, j]))
            for i in range(j + 1, ROWS):
                pivot[i, j] = pivot[i, j] * scale[j]
            for k in range(j + 1, ROWS):
                for i in range(k, ROWS):
                    pivot[i, k] = pivot[i, k] - pivot[i, j] * pivot[k, j]
        solved_left, solved_right = [], []
        for j in range(ROWS):
            a = jnp.broadcast_to(left[p][j : j + 1, :], spread)
            x = jnp.broadcast_to(right[p][j : j + 1, :], spread)
            for k in range(j):
                a = a - pivot[j, k] * solved_left[k]
                x = x - pivot[j, k] * solved_right[k]
            solved_left.append(a * scale[j])
            solved_right.append(x * scale[j])
        for q in range(p + 1, panels):
            below = []
            for j in range(ROWS):
                v = jnp.broadcast_to(left[q][:, at + j : at + j + 1], spread)
                for k in range(j):
                    v = v - pivot[j, k] * below[k]
                below.append(v * scale[j])
            for j in range(ROWS):
                left[q] = left[q] - below[j] * solved_left[j]
                right[q] = right[q] - below[j] * solved_right[j]
        line, _ = iotas(spread)
        kept_left, kept_right = solved_left[0], solved_right[0]
        for j in range(1, ROWS):
            kept_left = jnp.where(line == j, solved_left[j], kept_left)
            kept_right = jnp.where(line == j, solved_right[j], kept_right)
        left[p], right[p] = kept_left, kept_right
    inverse = jnp.concatenate(right, axis=0)
    for k in range(NEAR):
        parcels[k][0:width, :] = jnp.where(row >= column, inverse, stiff[k])
        diagonal = jnp.sum(jnp.where(row == column, stiff[k], 0.0), axis=0, keepdims=True)
        parcels[k][width:, :] = jnp.broadcast_to(diagonal, (ROWS, width))
    factor[0] = jnp.where(row <= column, jnp.concatenate(left, axis=0), 0.0).T


def transform_kernel(offset, projected, stiff_iface, *refs):
    parcels = refs[:NEAR]
    reduced, coupled, split, held, sent = refs[NEAR:]
    blocks, kept, width = projected.shape
    row, column = iotas((width, width))
    upper = jnp.zeros((width, width), F32)
    diagonal = jnp.zeros((1, width), F32)
    for k in range(NEAR):
        piece = parcels[k][0:width, :]
        high, low = halves(jnp.where(row >= column, piece, 0.0))
        split[k, :, 0:width] = high
        split[k, :, width:] = low
        upper = upper + jnp.where(row < column, piece, 0.0)
        diagonal = diagonal + parcels[k][width : width + 1, :]
    copies = []
    for first in range(0, blocks, GROUP):
        for b in range(first, first + GROUP):
            twice = jnp.concatenate([projected[b], projected[b]], axis=1)
            held[b] = dot(twice, split[offset[b]], (1, 1)).astype(BF16)
        some = pl.ds(first, GROUP)
        copies.append(
            pltpu.make_async_copy(held.at[some], coupled.at[some], sent.at[first // GROUP])
        )
        copies[-1].start()
    on_diagonal = jnp.where(row == column, diagonal, 0.0)
    reduced[0] = stiff_iface[0] - (upper + upper.T + on_diagonal)
    for copy in copies:
        copy.wait()


def in_smem():
    return pl.BlockSpec(memory_space=pltpu.SMEM)


def in_vmem():
    return pl.BlockSpec(memory_space=pltpu.VMEM)


def per_device(
    modes, eigenvalues, sub_size, row_offset, stiff_coupling, iface_offset, stiff_iface, lumped_mass
):
    blocks, picks, width = stiff_coupling.shape
    rows, kept = modes.shape
    span = rows // 2
    def array(*shape, dtype=F32):
        return jax.ShapeDtypeStruct(shape, dtype)

    def near(*shape, dtype=F32):
        return pltpu.VMEM(shape, dtype)

    anywhere = pl.BlockSpec(memory_space=pl.ANY)
    turned, *sums = pl.pallas_call(
        project_kernel,
        in_specs=[in_smem()] + [pl.BlockSpec(memory_space=pltpu.HBM)] * 5,
        out_specs=[in_vmem()] * (1 + NEAR),
        out_shape=[near(blocks, width, kept, dtype=BF16)] + [near(width, width)] * NEAR,
        scratch_shapes=[
            pltpu.SMEM(iface_offset.shape, jnp.int32),
            pltpu.VMEM(modes.shape, BF16),
            pltpu.VMEM(eigenvalues.shape, F32),
            pltpu.VMEM(row_offset.shape, jnp.int32),
            pltpu.VMEM(stiff_coupling.shape, BF16),
            pltpu.VMEM((span, kept), BF16),
            pltpu.VMEM((2, GROUP * picks, kept), BF16),
            pltpu.VMEM((NEAR, width, width), F32),
            pltpu.SemaphoreType.DMA((4 + PARTS,)),
        ],
        compiler_params=pltpu.CompilerParams(vmem_limit_bytes=VMEM_LIMIT),
        name="project",
    )(
        sub_size,
        *(
            pltpu.with_memory_space_constraint(x, pltpu.HBM)
            for x in (iface_offset, modes, eigenvalues, row_offset, stiff_coupling)
        ),
    )
    received = [sums[REACH]] + [passed_along(sums[d + REACH], "sub", d) for d in DISTANCES]
    projected, stiff = pl.pallas_call(
        stiffen_kernel,
        in_specs=[in_smem()] + [in_vmem()] * 2,
        out_specs=[in_vmem()] * 2,
        out_shape=[near(blocks, kept, width, dtype=BF16), near(NEAR, width, width)],
        compiler_params=pltpu.CompilerParams(vmem_limit_bytes=VMEM_LIMIT),
        name="stiffen",
    )(iface_offset, eigenvalues, turned)
    factor, *parcels = pl.pallas_call(
        factor_kernel,
        in_specs=[in_vmem()] * (NEAR + 2),
        out_specs=[in_vmem()] * (1 + NEAR),
        out_shape=[array(1, width, width)] + [near(width + ROWS, width)] * NEAR,
        compiler_params=pltpu.CompilerParams(vmem_limit_bytes=VMEM_LIMIT),
        name="factor",
    )(*received, lumped_mass, stiff)
    arrived = [
        parcels[REACH] if d == 0 else passed_along(parcels[REACH - d], "sub", -d)
        for d in range(-REACH, REACH + 1)
    ]
    reduced, coupled = pl.pallas_call(
        transform_kernel,
        in_specs=[in_smem()] + [in_vmem()] * (NEAR + 2),
        out_specs=[in_vmem(), anywhere],
        out_shape=[array(1, width, width), array(blocks, kept, width, dtype=BF16)],
        scratch_shapes=[
            pltpu.VMEM((NEAR, width, 2 * width), BF16),
            pltpu.VMEM((blocks, kept, width), BF16),
            pltpu.SemaphoreType.DMA((blocks // GROUP,)),
        ],
        compiler_params=pltpu.CompilerParams(vmem_limit_bytes=VMEM_LIMIT),
        name="transform",
    )(iface_offset, projected, stiff_iface, *arrived)
    return (reduced, factor, coupled)


def solution(mesh):
    placed = (
        P(("groups", "sub"), None),
        P(("groups", "sub"), None),
        P(("groups", "sub")),
        P(("groups", "sub"), None),
        P(("groups", "sub"), None, None),
        P(("groups", "sub")),
        P(("groups", "sub"), None, None),
        P(("groups", "sub"), None),
    )
    return jax.shard_map(
        per_device,
        mesh=mesh,
        in_specs=placed,
        out_specs=(
            P(("groups", "sub"), None, None),
            P(("groups", "sub"), None, None),
            P(("groups", "sub"), None, None),
        ),
        check_vma=False,
    )
```

```python
import jax
import jax.numpy as jnp
from jax import lax
from jax.experimental import pallas as pl
from jax.experimental.pallas import tpu as pltpu
from jax.sharding import PartitionSpec as P

REACH = 3
NEAR = 2 * REACH + 1
GROUP = 4
ROWS = 8
PARTS = 4
TILE = 16
VMEM_LIMIT = 24 << 20
F32 = jnp.float32
BF16 = jnp.bfloat16


def exchanges(length):
    group = REACH + 1
    if length % group or length < 2 * group:
        return [
            ([(i, (i + d) % length) for i in range(length)], [d] * group)
            for d in range(-REACH, REACH + 1)
            if d != 0
        ]
    plans = []
    for crossing in (((3, 0), (2, 1)), ((1, 0), (3, 2)), ((2, 0), (3, 1))):
        far = [0] * group
        for high, low in crossing:
            far[high] = group + low - high
            far[low] = high - low - group
        plans.append(far)
    for mask in range(1, group):
        plans.append([(k ^ mask) - k for k in range(group)])
    plans = [plans[k] for k in (2, 1, 0, 3, 4, 5)]
    return [
        ([(i, (i + far[i % group]) % length) for i in range(length)], far) for far in plans
    ]


def slots():
    place = lax.rem(lax.axis_index("sub"), REACH + 1)
    found = []
    for _, far in exchanges(lax.axis_size("sub")):
        slot = jnp.int32(far[0] + REACH)
        for k in range(1, REACH + 1):
            slot = jnp.where(place == k, far[k] + REACH, slot)
        found.append(slot)
    return found


def exchanged(x, pairs):
    return pltpu.with_memory_space_constraint(lax.ppermute(x, "sub", pairs), pltpu.VMEM)


def halves(x):
    high = x.astype(BF16)
    return high, (x - high.astype(F32)).astype(BF16)


def dot(a, b, contract=(1, 0)):
    return lax.dot_general(
        a, b, (((contract[0],), (contract[1],)), ((), ())), preferred_element_type=F32
    )


def iotas(shape):
    return (
        lax.broadcasted_iota(jnp.int32, shape, 0),
        lax.broadcasted_iota(jnp.int32, shape, 1),
    )


def pack(full):
    width = full.shape[1]
    half = width // 2
    row, column = iotas((half, width))
    low = full[half:]
    from_low = (column < half) | (column - half > row)
    diagonal = jnp.sum(jnp.where(column - half == row, low, 0.0), axis=0, keepdims=True)
    return (
        jnp.where(from_low, low, pltpu.roll(full[:half], half, 1)),
        jnp.broadcast_to(diagonal, (ROWS, width)),
    )


def unpack(packed, extra):
    half, width = packed.shape[0] - ROWS, packed.shape[1]
    row, column = iotas((half, width))
    low = packed[:half]
    top = pltpu.roll(low, half, 1)
    off = jnp.concatenate(
        [
            jnp.where((column < half) & (row > column), top, 0.0),
            jnp.where((column < half) | (column - half > row), low, 0.0),
        ],
        axis=0,
    )
    diagonal = jnp.concatenate(
        [
            jnp.where(row == column, top + extra, 0.0),
            jnp.where(column - half == row, packed[half : half + 1] + extra, 0.0),
        ],
        axis=0,
    )
    return off + off.T + diagonal


def project_kernel(
    size, offset, modes, eigen, row_offset, coupling, turned, offsets, inverse, *rest
):
    packed = rest[:NEAR]
    rows, values, wants, blocks_in, span_rows, picked, sums, arrived = rest[NEAR:]
    blocks, picks, width = coupling.shape
    span = span_rows.shape[0]
    part = rows.shape[0] // PARTS
    pairs = [(row_offset, wants), (offset, offsets), (eigen, values)]
    pairs += [
        (modes.at[pl.ds(k * part, part), :], rows.at[pl.ds(k * part, part), :])
        for k in range(PARTS)
    ]
    pairs.append((coupling, blocks_in))
    copies = [
        pltpu.make_async_copy(source, target, arrived.at[k])
        for k, (source, target) in enumerate(pairs)
    ]
    for copy in copies:
        copy.start()
    sums[...] = jnp.zeros_like(sums)
    _, place = iotas((picks, span))
    for copy in copies[:3]:
        copy.wait()
    wanted = (span - 1 - wants[...]).T
    inverse[...] = 1.0 / values[...]
    weight = inverse[...] * inverse[...]
    start = size[0] - span
    base = jnp.minimum(start // TILE * TILE, rows.shape[0] - span - TILE)
    for copy in copies[3:]:
        copy.wait()
    window = rows[pl.ds(pl.multiple_of(base, TILE), span + TILE), :].astype(F32)
    moved = pltpu.roll(window, span + TILE - (start - base), 0)
    span_rows[...] = moved[:span].astype(BF16)
    groups = blocks // GROUP
    for i in range(groups + 2):
        if i >= 2:
            for b in range((i - 2) * GROUP, (i - 1) * GROUP):
                block = turned[b]
                mass = halves(block.astype(F32) * weight)
                terms = dot(jnp.concatenate(mass, axis=0), block, (1, 1))
                sums[offsets[b]] += terms[:width] + terms[width:]
        if 1 <= i <= groups:
            for g in range(GROUP):
                b = (i - 1) * GROUP + g
                mine = picked[(i - 1) % 2, g * picks : (g + 1) * picks, :]
                turned[b] = dot(blocks_in[b].T, mine).astype(BF16)
        if i < groups:
            chosen = [
                jnp.where(place == wanted[:, b : b + 1], 1.0, 0.0).astype(BF16)
                for b in range(i * GROUP, (i + 1) * GROUP)
            ]
            picked[i % 2] = dot(jnp.concatenate(chosen, axis=0), span_rows[...]).astype(BF16)
    half = width // 2
    for message, slot in zip(packed, slots() + [REACH], strict=True):
        message[:half, :], message[half:, :] = pack(sums[slot])


def stiffen_kernel(offset, inverse, turned, projected, sums):
    width = sums.shape[1]
    sums[...] = jnp.zeros_like(sums)
    weight = inverse[...]
    for b in range(turned.shape[0]):
        block = turned[b]
        stiff = halves(block.astype(F32) * weight)
        terms = dot(jnp.concatenate(stiff, axis=0), block, (1, 1))
        sums[offset[b]] += terms[:width] + terms[width:]
        projected[b] = block.T


def factor_kernel(*refs):
    received = refs[:NEAR]
    lumped, stiff, factor = refs[NEAR : NEAR + 3]
    parcels = refs[NEAR + 3 :]
    width = lumped.shape[1]
    total = received[0][...]
    for piece in received[1:]:
        total = total + piece[...]
    row, column = iotas((width, width))
    mass = unpack(total, lumped[...])
    panels = width // ROWS
    work = [mass[p * ROWS : (p + 1) * ROWS] for p in range(panels)]
    spread = (ROWS, width)
    line, lane = iotas(spread)
    corners = []
    for p in range(panels):
        at = p * ROWS
        inside = (lane >= at) & (lane < at + ROWS)
        columns = [
            jnp.broadcast_to(work[p][:, at + j : at + j + 1], spread) for j in range(ROWS)
        ]
        pivot = {
            (i, j): jnp.broadcast_to(columns[j][i : i + 1, :], spread)
            for j in range(ROWS)
            for i in range(j, ROWS)
        }
        scale = []
        for j in range(0, ROWS, 2):
            first, cross = pivot[j, j], pivot[j + 1, j]
            determinant = first * pivot[j + 1, j + 1] - cross * cross
            root, both = lax.rsqrt(first), lax.rsqrt(determinant)
            scale += [root, both * (first * root)]
            pivot[j + 1, j] = cross * root
            shared = both * root
            for i in range(j + 2, ROWS):
                ahead = first * pivot[i, j + 1] - cross * pivot[i, j]
                pivot[i, j] = pivot[i, j] * root
                pivot[i, j + 1] = ahead * shared
            for k in range(j + 2, ROWS):
                for i in range(k, ROWS):
                    pivot[i, k] = (pivot[i, k] - pivot[i, j] * pivot[k, j]) - pivot[
                        i, j + 1
                    ] * pivot[k, j + 1]
        top = jnp.where(inside, jnp.where(lane - at == line, 1.0, 0.0), work[p])
        solved = []
        for j in range(ROWS):
            a = jnp.broadcast_to(top[j : j + 1, :], spread)
            for k in range(j):
                a = a - pivot[j, k] * solved[k]
            solved.append(a * scale[j])
        for q in range(p, panels):
            below = []
            for j in range(ROWS):
                v = jnp.broadcast_to(work[q][:, at + j : at + j + 1], spread)
                for k in range(j):
                    v = v - pivot[j, k] * below[k]
                below.append(v * scale[j])
            if q == p:
                corner = jnp.zeros(spread, F32)
                for j in range(ROWS):
                    corner = jnp.where((lane == at + j) & (line >= j), below[j], corner)
                corners.append(corner)
            else:
                left = jnp.where(inside, 0.0, work[q])
                for j in range(ROWS):
                    left = left - below[j] * solved[j]
                work[q] = left
        kept = solved[0]
        for j in range(1, ROWS):
            kept = jnp.where(line == j, solved[j], kept)
        work[p] = kept
    inverse = jnp.concatenate(work, axis=0)
    for parcel, slot in zip(parcels, slots() + [REACH], strict=True):
        mine = stiff[slot]
        parcel[0:width, :] = jnp.where(row >= column, inverse, mine)
        diagonal = jnp.sum(jnp.where(row == column, mine, 0.0), axis=0, keepdims=True)
        parcel[width:, :] = jnp.broadcast_to(diagonal, (ROWS, width))
    outer = jnp.where(row // ROWS < column // ROWS, inverse, 0.0)
    factor[0] = outer.T + jnp.concatenate(corners, axis=0)


def transform_kernel(offset, projected, stiff_iface, *refs):
    parcels = refs[:NEAR]
    reduced, coupled, split, held, sent = refs[NEAR:]
    blocks, kept, width = projected.shape
    row, column = iotas((width, width))
    upper = jnp.zeros((width, width), F32)
    diagonal = jnp.zeros((1, width), F32)
    for parcel, slot in zip(parcels, slots() + [REACH], strict=True):
        piece = parcel[0:width, :]
        high, low = halves(jnp.where(row >= column, piece, 0.0))
        split[slot, :, 0:width] = high
        split[slot, :, width:] = low
        upper = upper + jnp.where(row < column, piece, 0.0)
        diagonal = diagonal + parcel[width : width + 1, :]
    copies = []
    for first in range(0, blocks, GROUP):
        for b in range(first, first + GROUP):
            twice = jnp.concatenate([projected[b], projected[b]], axis=1)
            held[b] = dot(twice, split[offset[b]], (1, 1)).astype(BF16)
        some = pl.ds(first, GROUP)
        copies.append(
            pltpu.make_async_copy(held.at[some], coupled.at[some], sent.at[first // GROUP])
        )
        copies[-1].start()
    on_diagonal = jnp.where(row == column, diagonal, 0.0)
    reduced[0] = stiff_iface[0] - (upper + upper.T + on_diagonal)
    for copy in copies:
        copy.wait()


def in_smem():
    return pl.BlockSpec(memory_space=pltpu.SMEM)


def in_vmem():
    return pl.BlockSpec(memory_space=pltpu.VMEM)


def per_device(
    modes, eigenvalues, sub_size, row_offset, stiff_coupling, iface_offset, stiff_iface, lumped_mass
):
    blocks, picks, width = stiff_coupling.shape
    rows, kept = modes.shape
    span = rows // 2
    def array(*shape, dtype=F32):
        return jax.ShapeDtypeStruct(shape, dtype)

    def near(*shape, dtype=F32):
        return pltpu.VMEM(shape, dtype)

    anywhere = pl.BlockSpec(memory_space=pl.ANY)
    turned, offsets, inverse, *sums = pl.pallas_call(
        project_kernel,
        in_specs=[in_smem()] + [pl.BlockSpec(memory_space=pltpu.HBM)] * 5,
        out_specs=[in_vmem(), in_smem(), in_vmem()] + [in_vmem()] * NEAR,
        out_shape=[
            near(blocks, width, kept, dtype=BF16),
            pltpu.SMEM((blocks,), jnp.int32),
            near(1, kept),
        ]
        + [near(width // 2 + ROWS, width)] * NEAR,
        scratch_shapes=[
            pltpu.VMEM(modes.shape, BF16),
            pltpu.VMEM(eigenvalues.shape, F32),
            pltpu.VMEM(row_offset.shape, jnp.int32),
            pltpu.VMEM(stiff_coupling.shape, BF16),
            pltpu.VMEM((span, kept), BF16),
            pltpu.VMEM((2, GROUP * picks, kept), BF16),
            pltpu.VMEM((NEAR, width, width), F32),
            pltpu.SemaphoreType.DMA((4 + PARTS,)),
        ],
        compiler_params=pltpu.CompilerParams(vmem_limit_bytes=VMEM_LIMIT),
        name="project",
    )(
        sub_size,
        *(
            pltpu.with_memory_space_constraint(x, pltpu.HBM)
            for x in (iface_offset, modes, eigenvalues, row_offset, stiff_coupling)
        ),
    )
    plans = [pairs for pairs, _ in exchanges(lax.axis_size("sub"))]
    received = [exchanged(x, pairs) for x, pairs in zip(sums, plans)] + sums[-1:]
    projected, stiff = pl.pallas_call(
        stiffen_kernel,
        in_specs=[in_smem()] + [in_vmem()] * 2,
        out_specs=[in_vmem()] * 2,
        out_shape=[near(blocks, kept, width, dtype=BF16), near(NEAR, width, width)],
        compiler_params=pltpu.CompilerParams(vmem_limit_bytes=VMEM_LIMIT),
        name="stiffen",
    )(offsets, inverse, turned)
    factor, *parcels = pl.pallas_call(
        factor_kernel,
        in_specs=[in_vmem()] * (NEAR + 2),
        out_specs=[in_vmem()] * (1 + NEAR),
        out_shape=[array(1, width, width)] + [near(width + ROWS, width)] * NEAR,
        compiler_params=pltpu.CompilerParams(vmem_limit_bytes=VMEM_LIMIT),
        name="factor",
    )(*received, lumped_mass, stiff)
    arrived = [exchanged(x, pairs) for x, pairs in zip(parcels, plans)] + parcels[-1:]
    reduced, coupled = pl.pallas_call(
        transform_kernel,
        in_specs=[in_smem()] + [in_vmem()] * (NEAR + 2),
        out_specs=[in_vmem(), anywhere],
        out_shape=[array(1, width, width), array(blocks, kept, width, dtype=BF16)],
        scratch_shapes=[
            pltpu.VMEM((NEAR, width, 2 * width), BF16),
            pltpu.VMEM((blocks, kept, width), BF16),
            pltpu.SemaphoreType.DMA((blocks // GROUP,)),
        ],
        compiler_params=pltpu.CompilerParams(vmem_limit_bytes=VMEM_LIMIT),
        name="transform",
    )(offsets, projected, stiff_iface, *arrived)
    return (reduced, factor, coupled)


def solution(mesh):
    placed = (
        P(("groups", "sub"), None),
        P(("groups", "sub"), None),
        P(("groups", "sub")),
        P(("groups", "sub"), None),
        P(("groups", "sub"), None, None),
        P(("groups", "sub")),
        P(("groups", "sub"), None, None),
        P(("groups", "sub"), None),
    )
    return jax.shard_map(
        per_device,
        mesh=mesh,
        in_specs=placed,
        out_specs=(
            P(("groups", "sub"), None, None),
            P(("groups", "sub"), None, None),
            P(("groups", "sub"), None, None),
        ),
        check_vma=False,
    )
```

```python
import jax
import jax.numpy as jnp
from jax import lax
from jax.experimental import pallas as pl
from jax.experimental.pallas import tpu as pltpu
from jax.sharding import PartitionSpec as P

REACH = 3
NEAR = 2 * REACH + 1
GROUP = 4
ROWS = 8
PARTS = 4
CHUNK = 4
TILE = 16
VMEM_LIMIT = 24 << 20
F32 = jnp.float32
BF16 = jnp.bfloat16


def exchanges(length):
    group = REACH + 1
    if length % group or length < 2 * group:
        return [
            ([(i, (i + d) % length) for i in range(length)], [d] * group)
            for d in range(-REACH, REACH + 1)
            if d != 0
        ]
    plans = []
    for crossing in (((3, 0), (2, 1)), ((1, 0), (3, 2)), ((2, 0), (3, 1))):
        far = [0] * group
        for high, low in crossing:
            far[high] = group + low - high
            far[low] = high - low - group
        plans.append(far)
    for mask in range(1, group):
        plans.append([(k ^ mask) - k for k in range(group)])
    plans = [plans[k] for k in (2, 1, 0, 4, 5, 3)]
    return [
        ([(i, (i + far[i % group]) % length) for i in range(length)], far) for far in plans
    ]


def slots():
    place = lax.rem(lax.axis_index("sub"), REACH + 1)
    found = []
    for _, far in exchanges(lax.axis_size("sub")):
        slot = jnp.int32(far[0] + REACH)
        for k in range(1, REACH + 1):
            slot = jnp.where(place == k, far[k] + REACH, slot)
        found.append(slot)
    return found


def exchanged(x, pairs):
    return pltpu.with_memory_space_constraint(lax.ppermute(x, "sub", pairs), pltpu.VMEM)


def halves(x):
    high = x.astype(BF16)
    return high, (x - high.astype(F32)).astype(BF16)


def dot(a, b, contract=(1, 0)):
    return lax.dot_general(
        a, b, (((contract[0],), (contract[1],)), ((), ())), preferred_element_type=F32
    )


def iotas(shape):
    return (
        lax.broadcasted_iota(jnp.int32, shape, 0),
        lax.broadcasted_iota(jnp.int32, shape, 1),
    )


def pack(full):
    width = full.shape[1]
    half = width // 2
    row, column = iotas((half, width))
    low = full[half:]
    from_low = (column < half) | (column - half > row)
    diagonal = jnp.sum(jnp.where(column - half == row, low, 0.0), axis=0, keepdims=True)
    return (
        jnp.where(from_low, low, pltpu.roll(full[:half], half, 1)),
        jnp.broadcast_to(diagonal, (ROWS, width)),
    )


def unpack(packed, extra):
    half, width = packed.shape[0] - ROWS, packed.shape[1]
    row, column = iotas((half, width))
    low = packed[:half]
    top = pltpu.roll(low, half, 1)
    off = jnp.concatenate(
        [
            jnp.where((column < half) & (row > column), top, 0.0),
            jnp.where((column < half) | (column - half > row), low, 0.0),
        ],
        axis=0,
    )
    diagonal = jnp.concatenate(
        [
            jnp.where(row == column, top + extra, 0.0),
            jnp.where(column - half == row, packed[half : half + 1] + extra, 0.0),
        ],
        axis=0,
    )
    return off + off.T + diagonal


def project_kernel(
    size, offset, modes, eigen, row_offset, coupling, turned, offsets, inverse, *rest
):
    packed = rest[:NEAR]
    rows, values, wants, blocks_in, span_rows, chosen, picked, sums, arrived = rest[NEAR:]
    blocks, picks, width = coupling.shape
    span = span_rows.shape[0]
    start = size[0] - span
    base = jnp.minimum(start // TILE * TILE, modes.shape[0] - span - TILE)
    part = -(-(span + TILE) // (PARTS * TILE)) * TILE
    pairs = [(row_offset, wants), (eigen, values)]
    for first in range(0, span + TILE, part):
        some = min(part, span + TILE - first)
        source = modes.at[pl.ds(pl.multiple_of(base + first, TILE), some), :]
        pairs.append((source, rows.at[pl.ds(first, some), :]))
    pairs += [(offset, offsets), (coupling, blocks_in)]
    copies = [
        pltpu.make_async_copy(source, target, arrived.at[k])
        for k, (source, target) in enumerate(pairs)
    ]
    for copy in copies:
        copy.start()
    sums[...] = jnp.zeros_like(sums)
    _, place = iotas((picks, span))
    copies[0].wait()
    wanted = (span - 1 - wants[...]).T

    def choose(i):
        return jnp.concatenate(
            [
                jnp.where(place == wanted[:, b : b + 1], 1.0, 0.0).astype(BF16)
                for b in range(i * GROUP, (i + 1) * GROUP)
            ],
            axis=0,
        )

    for copy in copies[1:-2]:
        copy.wait()
    inverse[...] = 1.0 / values[...]
    weight = inverse[...] * inverse[...]
    moved = pltpu.roll(rows[...].astype(F32), span + TILE - (start - base), 0)
    span_rows[...] = moved[:span].astype(BF16)
    groups = blocks // GROUP
    for i in range(groups + 2):
        if i >= 2:
            for b in range((i - 2) * GROUP, (i - 1) * GROUP):
                block = turned[b]
                mass = halves(block.astype(F32) * weight)
                terms = dot(jnp.concatenate(mass, axis=0), block, (1, 1))
                sums[offsets[b]] += terms[:width] + terms[width:]
        if 1 <= i <= groups:
            for g in range(GROUP):
                b = (i - 1) * GROUP + g
                mine = picked[(i - 1) % 2, g * picks : (g + 1) * picks, :]
                turned[b] = dot(blocks_in[b].T, mine).astype(BF16)
        if i < groups:
            rows_of = choose(i)
            picked[i % 2] = dot(rows_of, span_rows[...]).astype(BF16)
        if i == 0:
            for copy in copies[-2:]:
                copy.wait()
    half = width // 2
    for message, slot in zip(packed, slots() + [REACH], strict=True):
        message[:half, :], message[half:, :] = pack(sums[slot])


def stiffen_kernel(offset, inverse, turned, projected, sums):
    width = sums.shape[1]
    sums[...] = jnp.zeros_like(sums)
    weight = inverse[...]
    for b in range(turned.shape[0]):
        block = turned[b]
        stiff = halves(block.astype(F32) * weight)
        terms = dot(jnp.concatenate(stiff, axis=0), block, (1, 1))
        sums[offset[b]] += terms[:width] + terms[width:]
        projected[b] = block.T


def factor_kernel(*refs):
    received = refs[:NEAR]
    lumped, stiff, factor = refs[NEAR : NEAR + 3]
    parcels = refs[NEAR + 3 :]
    width = lumped.shape[1]
    total = received[0][...]
    for piece in received[1:]:
        total = total + piece[...]
    row, column = iotas((width, width))
    mass = unpack(total, lumped[...])
    panels = width // ROWS
    work = [mass[p * ROWS : (p + 1) * ROWS] for p in range(panels)]
    spread = (ROWS, width)
    line, lane = iotas(spread)
    corners = []
    for p in range(panels):
        at = p * ROWS
        inside = (lane >= at) & (lane < at + ROWS)
        columns = [
            jnp.broadcast_to(work[p][:, at + j : at + j + 1], spread) for j in range(ROWS)
        ]
        pivot = {
            (i, j): jnp.broadcast_to(columns[j][i : i + 1, :], spread)
            for j in range(ROWS)
            for i in range(j, ROWS)
        }
        scale = []
        for j in range(0, ROWS, 2):
            first, cross = pivot[j, j], pivot[j + 1, j]
            determinant = first * pivot[j + 1, j + 1] - cross * cross
            root, both = lax.rsqrt(first), lax.rsqrt(determinant)
            scale += [root, both * (first * root)]
            pivot[j + 1, j] = cross * root
            shared = both * root
            for i in range(j + 2, ROWS):
                ahead = first * pivot[i, j + 1] - cross * pivot[i, j]
                pivot[i, j] = pivot[i, j] * root
                pivot[i, j + 1] = ahead * shared
            for k in range(j + 2, ROWS):
                for i in range(k, ROWS):
                    pivot[i, k] = (pivot[i, k] - pivot[i, j] * pivot[k, j]) - pivot[
                        i, j + 1
                    ] * pivot[k, j + 1]
        top = jnp.where(inside, jnp.where(lane - at == line, 1.0, 0.0), work[p])
        solved = []
        for j in range(ROWS):
            a = jnp.broadcast_to(top[j : j + 1, :], spread)
            for k in range(j):
                a = a - pivot[j, k] * solved[k]
            solved.append(a * scale[j])
        for q in range(p, panels):
            below = []
            for j in range(ROWS):
                v = jnp.broadcast_to(work[q][:, at + j : at + j + 1], spread)
                for k in range(j):
                    v = v - pivot[j, k] * below[k]
                below.append(v * scale[j])
            if q == p:
                corner = jnp.zeros(spread, F32)
                for j in range(ROWS):
                    corner = jnp.where((lane == at + j) & (line >= j), below[j], corner)
                corners.append(corner)
            else:
                left = jnp.where(inside, 0.0, work[q])
                for j in range(ROWS):
                    left = left - below[j] * solved[j]
                work[q] = left
        kept = solved[0]
        for j in range(1, ROWS):
            kept = jnp.where(line == j, solved[j], kept)
        work[p] = kept
    inverse = jnp.concatenate(work, axis=0)
    for parcel, slot in zip(parcels, slots() + [REACH], strict=True):
        mine = stiff[slot]
        parcel[0:width, :] = jnp.where(row >= column, inverse, mine)
        diagonal = jnp.sum(jnp.where(row == column, mine, 0.0), axis=0, keepdims=True)
        parcel[width:, :] = jnp.broadcast_to(diagonal, (ROWS, width))
    outer = jnp.where(row // ROWS < column // ROWS, inverse, 0.0)
    factor[0] = outer.T + jnp.concatenate(corners, axis=0)


def transform_kernel(offset, projected, stiff_iface, *refs):
    parcels = refs[:NEAR]
    reduced, coupled, split, held, sent = refs[NEAR:]
    blocks, kept, width = projected.shape
    row, column = iotas((width, width))
    upper = jnp.zeros((width, width), F32)
    diagonal = jnp.zeros((1, width), F32)
    for parcel, slot in zip(parcels, slots() + [REACH], strict=True):
        piece = parcel[0:width, :]
        high, low = halves(jnp.where(row >= column, piece, 0.0))
        split[slot, :, 0:width] = high
        split[slot, :, width:] = low
        upper = upper + jnp.where(row < column, piece, 0.0)
        diagonal = diagonal + parcel[width : width + 1, :]
    copies = []
    for first in range(0, blocks, CHUNK):
        for b in range(first, first + CHUNK):
            twice = jnp.concatenate([projected[b], projected[b]], axis=1)
            held[b] = dot(twice, split[offset[b]], (1, 1)).astype(BF16)
        some = pl.ds(first, CHUNK)
        copies.append(
            pltpu.make_async_copy(held.at[some], coupled.at[some], sent.at[first // CHUNK])
        )
        copies[-1].start()
    on_diagonal = jnp.where(row == column, diagonal, 0.0)
    reduced[0] = stiff_iface[0] - (upper + upper.T + on_diagonal)
    for copy in copies:
        copy.wait()


def in_smem():
    return pl.BlockSpec(memory_space=pltpu.SMEM)


def in_vmem():
    return pl.BlockSpec(memory_space=pltpu.VMEM)


def per_device(
    modes, eigenvalues, sub_size, row_offset, stiff_coupling, iface_offset, stiff_iface, lumped_mass
):
    blocks, picks, width = stiff_coupling.shape
    rows, kept = modes.shape
    span = rows // 2
    def array(*shape, dtype=F32):
        return jax.ShapeDtypeStruct(shape, dtype)

    def near(*shape, dtype=F32):
        return pltpu.VMEM(shape, dtype)

    anywhere = pl.BlockSpec(memory_space=pl.ANY)
    turned, offsets, inverse, *sums = pl.pallas_call(
        project_kernel,
        in_specs=[in_smem()] + [pl.BlockSpec(memory_space=pltpu.HBM)] * 5,
        out_specs=[in_vmem(), in_smem(), in_vmem()] + [in_vmem()] * NEAR,
        out_shape=[
            near(blocks, width, kept, dtype=BF16),
            pltpu.SMEM((blocks,), jnp.int32),
            near(1, kept),
        ]
        + [near(width // 2 + ROWS, width)] * NEAR,
        scratch_shapes=[
            pltpu.VMEM((span + TILE, kept), BF16),
            pltpu.VMEM(eigenvalues.shape, F32),
            pltpu.VMEM(row_offset.shape, jnp.int32),
            pltpu.VMEM(stiff_coupling.shape, BF16),
            pltpu.VMEM((span, kept), BF16),
            pltpu.VMEM((GROUP * picks, span), BF16),
            pltpu.VMEM((2, GROUP * picks, kept), BF16),
            pltpu.VMEM((NEAR, width, width), F32),
            pltpu.SemaphoreType.DMA((4 + PARTS,)),
        ],
        compiler_params=pltpu.CompilerParams(vmem_limit_bytes=VMEM_LIMIT),
        name="project",
    )(
        sub_size,
        *(
            pltpu.with_memory_space_constraint(x, pltpu.HBM)
            for x in (iface_offset, modes, eigenvalues, row_offset, stiff_coupling)
        ),
    )
    plans = [pairs for pairs, _ in exchanges(lax.axis_size("sub"))]
    received = [exchanged(x, pairs) for x, pairs in zip(sums, plans)] + sums[-1:]
    projected, stiff = pl.pallas_call(
        stiffen_kernel,
        in_specs=[in_smem()] + [in_vmem()] * 2,
        out_specs=[in_vmem()] * 2,
        out_shape=[near(blocks, kept, width, dtype=BF16), near(NEAR, width, width)],
        compiler_params=pltpu.CompilerParams(vmem_limit_bytes=VMEM_LIMIT),
        name="stiffen",
    )(offsets, inverse, turned)
    factor, *parcels = pl.pallas_call(
        factor_kernel,
        in_specs=[in_vmem()] * (NEAR + 2),
        out_specs=[in_vmem()] * (1 + NEAR),
        out_shape=[array(1, width, width)] + [near(width + ROWS, width)] * NEAR,
        compiler_params=pltpu.CompilerParams(vmem_limit_bytes=VMEM_LIMIT),
        name="factor",
    )(*received, lumped_mass, stiff)
    arrived = [exchanged(x, pairs) for x, pairs in zip(parcels, plans)] + parcels[-1:]
    reduced, coupled = pl.pallas_call(
        transform_kernel,
        in_specs=[in_smem()] + [in_vmem()] * (NEAR + 2),
        out_specs=[in_vmem(), anywhere],
        out_shape=[array(1, width, width), array(blocks, kept, width, dtype=BF16)],
        scratch_shapes=[
            pltpu.VMEM((NEAR, width, 2 * width), BF16),
            pltpu.VMEM((blocks, kept, width), BF16),
            pltpu.SemaphoreType.DMA((blocks // CHUNK,)),
        ],
        compiler_params=pltpu.CompilerParams(vmem_limit_bytes=VMEM_LIMIT),
        name="transform",
    )(offsets, projected, stiff_iface, *arrived)
    return (reduced, factor, coupled)


def solution(mesh):
    placed = (
        P(("groups", "sub"), None),
        P(("groups", "sub"), None),
        P(("groups", "sub")),
        P(("groups", "sub"), None),
        P(("groups", "sub"), None, None),
        P(("groups", "sub")),
        P(("groups", "sub"), None, None),
        P(("groups", "sub"), None),
    )
    return jax.shard_map(
        per_device,
        mesh=mesh,
        in_specs=placed,
        out_specs=(
            P(("groups", "sub"), None, None),
            P(("groups", "sub"), None, None),
            P(("groups", "sub"), None, None),
        ),
        check_vma=False,
    )
```
